1024 devices in a mesh: dom: 64 (over z, core), grp: 16 (over y, x).
Axes of the slice: x: 4, y: 4, z: 32, core: 2. Of those that a mesh axis runs over, the one named last changes fastest.
Arguments:
- forcing: float32 [12288, 135], P(('dom', 'grp')), may hold values from -6 to 6
- diag_blocks: bfloat16 [12288, 135, 135], P(('dom', 'grp')), as said below
- off_blocks: bfloat16 [12288, 6, 135, 135], P(('dom', 'grp')), may hold values from -0.125 to 0.125
- precond: bfloat16 [12288, 135, 135], P(('dom', 'grp')), as said below
- face_part: int32 [6, 12288], P(None, ('dom', 'grp')), may hold values from -1 to 63, as said below
- face_slot: int32 [6, 12288], P(None, ('dom', 'grp')), may hold values from 0 to 191, as said below
- row_perm: int32 [64, 192], P('dom'), may hold values from 0 to 191, as said below
Outputs:
- adjoint: float32 [12288, 135], P(('dom', 'grp'))
- residual: float32 [12288, 135], P(('dom', 'grp'))
The draws below stay inside these ranges and needn't reach their ends.
Inputs may be any that keep to these rules, and one draw needn't show every extreme that they name: `face_part`: each entry is -1 (a wall) or the partition of the face's neighbour, which is the element's own partition or the one just below or just above it in number; no face points below partition 0 or above 63. `face_slot`: block row of the neighbour in its own partition; read only where face_part is not -1. `row_perm`: each row is a permutation of 0 to 191. `diag_blocks`: dominant diagonal of 1 to 2 on every block. `precond`: dominant diagonal of 0.4 to 0.8 on every block.
All inputs are finite; a program needn't handle non-finite values.
Results may differ from the reference program's by a relative error of at most 0.012.
The reference program's roundings to bfloat16 on the way count: a program that leaves them out, or rounds other values in their place, can miss the bound.
Values sent between devices are 32-bit elements; how exact they have to be, the bound alone decides.
No kernel may reach another device: no remote copies, remote signals or barrier semaphores. Data moves between devices by JAX's collectives and lax.ppermute only.
A program may use at most 32 MiB of HBM per device.

```python
import jax
import jax.numpy as jnp
from jax import lax

NODE = 135
FACES = 6
ITERS = 2
P_ELEMS = 192
PARTS_SIZE = 64
ELEMS = 12288


def dominant_blocks(key, low, high, spread):
    first, second = jax.random.split(key)
    diag_values = jax.random.uniform(first, (ELEMS, NODE), jnp.float32, low, high)
    scatter = jax.random.normal(second, (ELEMS, NODE, NODE), jnp.float32) * (spread / NODE ** 0.5)
    identity = jnp.eye(NODE, dtype=jnp.float32)
    return (scatter * (1.0 - identity) + identity * diag_values[:, :, None]).astype(jnp.bfloat16)


def draw_diag_blocks(key, part):
    return dominant_blocks(jax.random.fold_in(key, 11), 1.0, 2.0, 0.4)


def draw_precond(key, part):
    return dominant_blocks(jax.random.fold_in(key, 23), 0.4, 0.8, 0.2)


def draw_face_part(key, part):
    codes = jax.random.randint(jax.random.fold_in(key, 37), (FACES, ELEMS), 0, 12)
    owner = (jnp.arange(ELEMS, dtype=jnp.int32) // P_ELEMS)[None, :]
    offset = jnp.where(codes < 2, -1, jnp.where(codes < 4, 1, 0))
    target = owner + offset
    outside = (target < 0) | (target >= PARTS_SIZE) | (codes == 11)
    return jnp.where(outside, -1, target).astype(jnp.int32)


def draw_face_slot(key, part):
    slots = jax.random.randint(jax.random.fold_in(key, 41), (FACES, ELEMS), 0, P_ELEMS)
    first_rows = (jnp.arange(ELEMS, dtype=jnp.int32) % P_ELEMS == 0)[None, :]
    face_index = jnp.arange(FACES, dtype=jnp.int32)[:, None]
    slots = jnp.where(first_rows & (face_index == 0), P_ELEMS - 1, slots)
    slots = jnp.where(first_rows & (face_index == 1), 0, slots)
    return slots.astype(jnp.int32)


def draw_row_perm(key, part):
    table = jnp.tile(jnp.arange(P_ELEMS, dtype=jnp.int32)[None, :], (PARTS_SIZE, 1))
    return jax.random.permutation(jax.random.fold_in(key, 53), table, axis=1, independent=True).astype(jnp.int32)


def block_scale(stream_key, dims, cuts, low, high):
    def one(position, parts):
        steps = jax.random.uniform(jax.random.fold_in(jax.random.fold_in(stream_key, 6), position), (parts,), jnp.float32, low / len(cuts), high / len(cuts))
        return jnp.repeat(jnp.exp(steps), dims[position] // parts).reshape((-1,) + (1,) * (len(dims) - position - 1))

    gain = one(*cuts[0])
    for cut in cuts[1:]:
        gain = gain * one(*cut)
    return gain


def scatter_about(own_key, shape, deviation, limit, pieces=(), held_as=jnp.bfloat16):
    entries = jax.random.normal(own_key, shape, jnp.float32) * deviation
    if len(pieces) > 0:
        entries = block_scale(own_key, shape, pieces, -0.22, 0.18) * entries
    return jnp.clip(entries, min=-limit, max=limit).astype(held_as)


def setup_inputs(seed: int = 0) -> dict:
    streams_of = jax.random.split(jax.random.key(seed), 8)
    return {
        "forcing": scatter_about(streams_of[0], (ELEMS, NODE), 1.0, 6.0, ((0, 1024),), jnp.float32),
        "diag_blocks": draw_diag_blocks(jax.random.fold_in(streams_of[7], 71), 0),
        "off_blocks": scatter_about(streams_of[2], (ELEMS, FACES, NODE, NODE), (15 * NODE) ** -0.5, 0.125, ((0, 1024),)),
        "precond": draw_precond(jax.random.fold_in(streams_of[7], 71), 0),
        "face_part": draw_face_part(jax.random.fold_in(streams_of[7], 71), 0),
        "face_slot": draw_face_slot(jax.random.fold_in(streams_of[7], 71), 0),
        "row_perm": draw_row_perm(jax.random.fold_in(streams_of[7], 71), 0),
    }


def transposed(adjoint, diag_blocks, off_blocks, targets):
    adjoint_b = adjoint.astype(jnp.bfloat16)
    diag_split = diag_blocks.reshape(PARTS_SIZE, P_ELEMS, NODE, NODE)
    off_split = off_blocks.reshape(PARTS_SIZE, P_ELEMS, FACES, NODE, NODE)
    vec_split = adjoint_b.reshape(PARTS_SIZE, P_ELEMS, NODE)

    def per_part(items):
        diag_part, off_part, vec_part = items
        vec_float = vec_part.astype(jnp.float32)
        diag_term = jnp.einsum("eij,ei->ej", diag_part.astype(jnp.float32), vec_float)
        face_term = jnp.einsum("ekij,ei->kej", off_part.astype(jnp.float32), vec_float)
        return diag_term, face_term

    diag_term, face_term = lax.map(per_part, (diag_split, off_split, vec_split))
    summed = jax.ops.segment_sum(face_term.reshape(-1, NODE), targets.reshape(-1), num_segments=ELEMS + 1)
    return diag_term.reshape(ELEMS, NODE) + summed[:ELEMS]


def apply_precond(precond, vector):
    return jnp.einsum("eij,ei->ej", precond.astype(jnp.float32), vector.astype(jnp.bfloat16).astype(jnp.float32))


def reference(forcing, diag_blocks, off_blocks, precond, face_part, face_slot, row_perm):
    part_of = face_part.reshape(FACES, PARTS_SIZE, P_ELEMS).transpose(1, 0, 2)
    slot_of = face_slot.reshape(FACES, PARTS_SIZE, P_ELEMS).transpose(1, 0, 2)
    safe_part = jnp.maximum(part_of, 0)
    stored = row_perm[safe_part, slot_of]
    targets = jnp.where(part_of < 0, ELEMS, safe_part * P_ELEMS + stored).astype(jnp.int32)
    adjoint = apply_precond(precond, forcing)
    residual = forcing
    for step in range(ITERS):
        residual = forcing - transposed(adjoint, diag_blocks, off_blocks, targets)
        adjoint = adjoint + apply_precond(precond, residual)
    return adjoint, residual
```

```python
import jax
import jax.numpy as jnp
from jax import lax
from jax.sharding import PartitionSpec as P

ITERS = 2
LANES = 256
SLOT_ROWS = 16


def passed_along(block, axis, distance):
    devices = range(lax.axis_size(axis))
    route = [(i - distance, i) for i in devices if i - distance in devices]
    return lax.ppermute(block, axis, route)


def apply_blocks(blocks, vector):
    return jnp.einsum(
        "eij,ei->ej", blocks, vector.astype(jnp.bfloat16), preferred_element_type=jnp.float32
    )


def shards(forcing, diag_blocks, off_blocks, precond, face_part, face_slot, row_perm):
    local_rows = forcing.shape[0]
    node_width = forcing.shape[1]
    group_size = lax.axis_size("grp")
    part_rows = local_rows * group_size
    my_part = lax.axis_index("dom")
    perm_row = row_perm[0]
    offset = face_part - my_part
    dest = (offset + 1) * part_rows + face_slot
    dest = jnp.where(face_part < 0, -1, dest).reshape(-1)
    scatter_table = (dest[:, None] == jnp.arange(3 * part_rows, dtype=jnp.int32)[None, :]).astype(
        jnp.float32
    )
    place = (perm_row // local_rows) * SLOT_ROWS + perm_row % local_rows
    place_table = (
        jnp.arange(group_size * SLOT_ROWS, dtype=jnp.int32)[:, None] == place[None, :]
    ).astype(jnp.float32)
    adjoint = apply_blocks(precond, forcing)
    residual = forcing
    for step in range(ITERS):
        adjoint_b = adjoint.astype(jnp.bfloat16)
        face_term = jnp.einsum(
            "ekij,ei->kej", off_blocks, adjoint_b, preferred_element_type=jnp.float32
        )
        face_term = face_term.reshape(-1, node_width)
        face_term = jnp.pad(face_term, ((0, 0), (0, LANES - node_width)))
        buffers = jnp.einsum("fp,fn->pn", scatter_table, face_term, precision=lax.Precision.HIGHEST)
        buffers = buffers.reshape(3, part_rows, LANES)
        from_prev = passed_along(buffers[2], "dom", 1)
        from_next = passed_along(buffers[0], "dom", -1)
        total = buffers[1] + from_prev + from_next
        outgoing = jnp.dot(place_table, total, precision=lax.Precision.HIGHEST)
        incoming = lax.all_to_all(
            outgoing.reshape(group_size, SLOT_ROWS, LANES), "grp", split_axis=0, concat_axis=0
        )
        gathered = jnp.sum(incoming, axis=0)[:local_rows, :node_width]
        diag_term = apply_blocks(diag_blocks, adjoint)
        residual = forcing - (diag_term + gathered)
        adjoint = adjoint + apply_blocks(precond, residual)
    return (adjoint, residual)


def solution(mesh):
    return jax.shard_map(
        shards,
        mesh=mesh,
        in_specs=(
            P(("dom", "grp"), None),
            P(("dom", "grp"), None, None),
            P(("dom", "grp"), None, None, None),
            P(("dom", "grp"), None, None),
            P(None, ("dom", "grp")),
            P(None, ("dom", "grp")),
            P("dom", None),
        ),
        out_specs=(P(("dom", "grp"), None), P(("dom", "grp"), None)),
        check_vma=False,
    )
```

```python
import jax
import jax.numpy as jnp
from jax import lax
from jax.experimental import pallas as pl
from jax.experimental.pallas import tpu as pltpu
from jax.sharding import PartitionSpec as P

LANES = 128
WIDE = 256
PAD_ROWS = 16
TAIL_STEP = 8
F32 = jnp.float32
BF16 = jnp.bfloat16
PARAMS = pltpu.CompilerParams(vmem_limit_bytes=16 * 1024 * 1024)


def iota(shape, axis):
    return lax.broadcasted_iota(jnp.int32, shape, axis)


def split(values):
    high = values.astype(BF16)
    return high, (values - high.astype(F32)).astype(BF16)


def select_rows(table, values):
    high, low = split(values)
    return jnp.dot(table, high, preferred_element_type=F32) + jnp.dot(
        table, low, preferred_element_type=F32
    )


def block_products(vector_ref, blocks_ref, out_ref):
    elements, width = blocks_ref.shape[0], blocks_ref.shape[-1]
    for e in range(elements):
        row = vector_ref[e : e + 1, 0:width].astype(BF16)
        out_ref[e : e + 1, 0:width] = jnp.dot(row, blocks_ref[e], preferred_element_type=F32)


def face_products(adjoint_ref, blocks_ref, faces_ref, arrived):
    faces_ref[...] = jnp.zeros(faces_ref.shape, F32)
    elements, faces, width = blocks_ref.shape[0], blocks_ref.shape[1], blocks_ref.shape[-1]
    for e in range(elements):
        row = adjoint_ref[e : e + 1, 0:width].astype(BF16)
        arrived(e)
        for k in range(faces):
            at = k * PAD_ROWS + e
            faces_ref[at : at + 1, 0:width] = jnp.dot(
                row, blocks_ref[e, k], preferred_element_type=F32
            )


def face_targets(part_ref, slot_ref, my_part, part_rows):
    faces, elements = part_ref.shape
    part, slot = part_ref[...], slot_ref[...]
    offset = part - my_part
    towards_chip = 1 - 2 * (my_part & 1)
    section = jnp.where(offset == 0, 0, jnp.where(offset == towards_chip, 1, 2))
    target = jnp.where(part < 0, -1, section * part_rows + slot)
    target = jnp.pad(target, ((0, 0), (0, LANES - elements)))
    row = jnp.zeros((1, LANES), jnp.int32)
    lane = iota((1, LANES), 1)
    for k in range(faces):
        moved = pltpu.roll(target[k : k + 1], k * PAD_ROWS, 1)
        row = jnp.where(lane // PAD_ROWS == k, moved, row)
    real = jnp.logical_and(lane < faces * PAD_ROWS, lane % PAD_ROWS < elements)
    return jnp.where(real, row, -1)


def sent_rows(target_row, faces_ref, section, rows):
    count = faces_ref.shape[0]
    table = iota((rows, count), 0) + section * rows == target_row[:, 0:count]
    return select_rows(table.astype(BF16), faces_ref[...])


def first_kernel(
    my_part_ref, forcing_hbm, precond_hbm, off_hbm, diag_hbm, part_hbm, slot_hbm, perm_hbm,
    adjoint_ref, faces_ref, target_ref, next_ref, chip_ref,
    forcing_ref, precond_ref, kept_ref, diag_ref, perm_ref, part_ref, slot_ref, sems, off_sems,
):
    rows = chip_ref.shape[0]
    whole = [
        pltpu.make_async_copy(source, target, sems.at[i])
        for i, (source, target) in enumerate(
            (
                (forcing_hbm, forcing_ref),
                (precond_hbm, precond_ref),
                (part_hbm, part_ref),
                (slot_hbm, slot_ref),
                (perm_hbm, perm_ref),
                (diag_hbm, diag_ref),
            )
        )
    ]
    by_element = [
        pltpu.make_async_copy(off_hbm.at[e], kept_ref.at[e], off_sems.at[e])
        for e in range(off_hbm.shape[0])
    ]
    for copy in whole[:5] + by_element + whole[5:]:
        copy.start()
    adjoint_ref[...] = jnp.zeros(adjoint_ref.shape, F32)
    for copy in whole[:2]:
        copy.wait()
    block_products(forcing_ref, precond_ref, adjoint_ref)
    for copy in whole[2:5]:
        copy.wait()
    target = face_targets(part_ref, slot_ref, my_part_ref[0], rows)
    target_ref[...] = target
    face_products(adjoint_ref, kept_ref, faces_ref, lambda e: by_element[e].wait())
    next_ref[...] = sent_rows(target, faces_ref, 2, rows)
    chip_ref[...] = sent_rows(target, faces_ref, 1, rows)
    whole[5].wait()


def own_part(forcing_ref, adjoint_ref, diag_ref, faces_ref, target_ref, own_ref, rest_ref):
    elements, width = forcing_ref.shape
    own_ref[...] = sent_rows(target_ref[...], faces_ref, 0, own_ref.shape[0])
    rest_ref[...] = jnp.zeros(rest_ref.shape, F32)
    block_products(adjoint_ref, diag_ref, rest_ref)
    rest_ref[0:elements, 0:width] = forcing_ref[...] - rest_ref[0:elements, 0:width]


def own_kernel_first(
    forcing_ref, adjoint_ref, diag_ref, faces_ref, target_ref, perm_ref, own_ref, rest_ref, place_ref
):
    elements = forcing_ref.shape[0]
    perm = perm_ref[...]
    rank = (perm * (65536 // elements + 1)) >> 16
    place = rank * PAD_ROWS + perm - rank * elements
    place_ref[...] = (iota(place_ref.shape, 0) == place).astype(F32).astype(BF16)
    own_part(forcing_ref, adjoint_ref, diag_ref, faces_ref, target_ref, own_ref, rest_ref)


def pack_kernel(own_ref, chip_ref, next_ref, place_ref, out_ref):
    elements_step = TAIL_STEP
    ranks = out_ref.shape[0]
    total = own_ref[...] + chip_ref[...] + next_ref[...]
    placed = select_rows(place_ref[...], total)
    main, tail = placed[:, 0:LANES], placed[:, LANES:WIDE]
    moved = pltpu.roll(tail, 0, 1, stride=elements_step, stride_axis=0)
    row = iota((PAD_ROWS, LANES), 0)
    for r in range(ranks):
        at = slice(r * PAD_ROWS, (r + 1) * PAD_ROWS)
        packed = jnp.sum(moved[at], axis=0, keepdims=True)
        out_ref[r] = jnp.where(row == PAD_ROWS - 4, packed, main[at])


def gathered_rows(arrived_ref, width):
    total = arrived_ref[0]
    for r in range(1, arrived_ref.shape[0]):
        total = total + arrived_ref[r]
    packed = total[PAD_ROWS - 4 : PAD_ROWS - 3]
    tail = jnp.broadcast_to(packed, (PAD_ROWS, LANES))
    row = iota((PAD_ROWS, LANES), 0)
    for r in range(1, PAD_ROWS - 4):
        tail = jnp.where(row == r, pltpu.roll(packed, LANES - TAIL_STEP * r, 1), tail)
    tail = jnp.where(iota((PAD_ROWS, LANES), 1) < width - LANES, tail, 0.0)
    return jnp.concatenate([total, tail], axis=1)


def next_kernel(
    arrived_ref, rest_ref, before_ref, precond_ref, blocks_ref, target_ref,
    adjoint_ref, faces_ref, next_ref, chip_ref, residual_ref,
):
    width = precond_ref.shape[-1]
    rows = chip_ref.shape[0]
    residual_ref[...] = rest_ref[...] - gathered_rows(arrived_ref, width)
    adjoint_ref[...] = jnp.zeros(adjoint_ref.shape, F32)
    block_products(residual_ref, precond_ref, adjoint_ref)
    adjoint_ref[...] = before_ref[...] + adjoint_ref[...]
    face_products(adjoint_ref, blocks_ref, faces_ref, lambda e: None)
    target = target_ref[...]
    next_ref[...] = sent_rows(target, faces_ref, 2, rows)
    chip_ref[...] = sent_rows(target, faces_ref, 1, rows)


def last_kernel(
    arrived_ref, rest_ref, before_ref, precond_ref, adjoint_ref, residual_ref, held_ref, sum_ref
):
    elements, width = residual_ref.shape
    held_ref[...] = rest_ref[...] - gathered_rows(arrived_ref, width)
    residual_ref[...] = held_ref[0:elements, 0:width]
    block_products(held_ref, precond_ref, sum_ref)
    adjoint_ref[...] = before_ref[0:elements, 0:width] + sum_ref[0:elements, 0:width]


def in_hbm(*arrays):
    return [pltpu.with_memory_space_constraint(a, pltpu.HBM) for a in arrays]


def cost(flops):
    return pl.CostEstimate(flops=flops, bytes_accessed=1 << 20, transcendentals=0)


def make_calls(elements, faces, width, ranks):
    part_rows = elements * ranks
    vector = pltpu.VMEM((PAD_ROWS, WIDE), F32)
    sent = pltpu.VMEM((part_rows, WIDE), F32)
    face_rows = pltpu.VMEM((faces * PAD_ROWS, WIDE), F32)
    target = pltpu.VMEM((1, LANES), jnp.int32)
    hbm = pl.BlockSpec(memory_space=pltpu.HBM)
    smem = pl.BlockSpec(memory_space=pltpu.SMEM)
    out = jax.ShapeDtypeStruct((elements, width), F32)
    blocks = pltpu.VMEM((elements, width, width), BF16)
    kept = (
        pltpu.VMEM((elements, width), F32),
        blocks,
        pltpu.VMEM((elements, faces, width, width), BF16),
        blocks,
        pltpu.VMEM((1, part_rows), jnp.int32),
    )
    indices = pltpu.VMEM((faces, elements), jnp.int32)
    first = pl.pallas_call(
        first_kernel,
        out_shape=(vector, face_rows, target, sent, sent, *kept),
        in_specs=[smem] + [hbm] * 7,
        scratch_shapes=[
            indices,
            indices,
            pltpu.SemaphoreType.DMA((6,)),
            pltpu.SemaphoreType.DMA((elements,)),
        ],
        compiler_params=PARAMS,
        name="first",
    )
    own_first = pl.pallas_call(
        own_kernel_first,
        out_shape=(sent, vector, pltpu.VMEM((ranks * PAD_ROWS, part_rows), BF16)),
        compiler_params=PARAMS,
        cost_estimate=cost(10**9),
        name="own_first",
    )
    own_next = pl.pallas_call(
        own_part,
        out_shape=(sent, vector),
        compiler_params=PARAMS,
        cost_estimate=cost(10**9),
        name="own_next",
    )
    pack = pl.pallas_call(
        pack_kernel,
        out_shape=pltpu.VMEM((ranks, PAD_ROWS, LANES), F32),
        compiler_params=PARAMS,
        name="pack",
    )
    following = pl.pallas_call(
        next_kernel,
        out_shape=(vector, face_rows, sent, sent),
        scratch_shapes=[pltpu.VMEM((PAD_ROWS, WIDE), F32)],
        compiler_params=PARAMS,
        name="following",
    )
    last = pl.pallas_call(
        last_kernel,
        out_shape=(out, out),
        scratch_shapes=[pltpu.VMEM((PAD_ROWS, WIDE), F32)] * 2,
        compiler_params=PARAMS,
        name="last",
    )
    return first, own_first, own_next, pack, following, last


def shards(forcing, diag_blocks, off_blocks, precond, face_part, face_slot, row_perm):
    elements, width = forcing.shape
    faces = face_part.shape[0]
    ranks = lax.axis_size("grp")
    parts = lax.axis_size("dom")
    first, own_first, own_next, pack, following, last = make_calls(elements, faces, width, ranks)
    my_part = lax.axis_index("dom").astype(jnp.int32).reshape(1)
    on_chip = [(p, p ^ 1) for p in range(parts)]
    across = [(p, ((p + 1) ^ 1) - 1) for p in range(1, parts - 1)]

    def exchange(beyond, chip):
        from_beyond = lax.ppermute(beyond, "dom", across)
        return from_beyond, lax.ppermute(chip, "dom", on_chip)

    adjoint, face_rows, target, beyond, chip, forcing, precond, kept, diag_blocks, perm = first(
        my_part,
        *in_hbm(forcing, precond, off_blocks, diag_blocks, face_part, face_slot, row_perm),
    )
    from_beyond, from_chip = exchange(beyond, chip)
    own, rest, place = own_first(forcing, adjoint, diag_blocks, face_rows, target, perm)
    arrived = lax.all_to_all(pack(own, from_chip, from_beyond, place), "grp", 0, 0)
    adjoint, face_rows, beyond, chip = following(arrived, rest, adjoint, precond, kept, target)
    from_beyond, from_chip = exchange(beyond, chip)
    own, rest = own_next(forcing, adjoint, diag_blocks, face_rows, target)
    arrived = lax.all_to_all(pack(own, from_chip, from_beyond, place), "grp", 0, 0)
    return last(arrived, rest, adjoint, precond)


def solution(mesh):
    return jax.shard_map(
        shards,
        mesh=mesh,
        in_specs=(
            P(("dom", "grp"), None),
            P(("dom", "grp"), None, None),
            P(("dom", "grp"), None, None, None),
            P(("dom", "grp"), None, None),
            P(None, ("dom", "grp")),
            P(None, ("dom", "grp")),
            P("dom", None),
        ),
        out_specs=(P(("dom", "grp"), None), P(("dom", "grp"), None)),
        check_vma=False,
    )
```

```python
import functools

import jax
import jax.numpy as jnp
from jax import lax
from jax.experimental import pallas as pl
from jax.experimental.pallas import tpu as pltpu
from jax.sharding import PartitionSpec as P

LANES = 128
WIDE = 256
PAD_ROWS = 16
TAIL_STEP = 8
F32 = jnp.float32
BF16 = jnp.bfloat16
PARAMS = pltpu.CompilerParams(vmem_limit_bytes=16 * 1024 * 1024)


def iota(shape, axis):
    return lax.broadcasted_iota(jnp.int32, shape, axis)


def split(values):
    high = values.astype(BF16)
    return high, (values - high.astype(F32)).astype(BF16)


def select_rows(table, values):
    high, low = split(values)
    return jnp.dot(table, high, preferred_element_type=F32) + jnp.dot(
        table, low, preferred_element_type=F32
    )


def block_products(vector_ref, blocks_ref, out_ref):
    elements, width = blocks_ref.shape[0], blocks_ref.shape[-1]
    for e in range(elements):
        row = vector_ref[e : e + 1, 0:width].astype(BF16)
        out_ref[e : e + 1, 0:width] = jnp.dot(row, blocks_ref[e], preferred_element_type=F32)


def face_products(adjoint_ref, blocks_ref, faces_ref, arrived):
    faces_ref[...] = jnp.zeros(faces_ref.shape, F32)
    elements, faces, width = blocks_ref.shape[0], blocks_ref.shape[1], blocks_ref.shape[-1]
    for e in range(elements):
        row = adjoint_ref[e : e + 1, 0:width].astype(BF16)
        arrived(e)
        for k in range(faces):
            at = k * PAD_ROWS + e
            faces_ref[at : at + 1, 0:width] = jnp.dot(
                row, blocks_ref[e, k], preferred_element_type=F32
            )


def face_targets(part_ref, slot_ref, my_part, part_rows):
    faces, elements = part_ref.shape
    part, slot = part_ref[...], slot_ref[...]
    offset = part - my_part
    towards_chip = 1 - 2 * (my_part & 1)
    section = jnp.where(offset == 0, 0, jnp.where(offset == towards_chip, 1, 2))
    target = jnp.where(part < 0, -1, section * part_rows + slot)
    target = jnp.pad(target, ((0, 0), (0, LANES - elements)))
    row = jnp.zeros((1, LANES), jnp.int32)
    lane = iota((1, LANES), 1)
    for k in range(faces):
        moved = pltpu.roll(target[k : k + 1], k * PAD_ROWS, 1)
        row = jnp.where(lane // PAD_ROWS == k, moved, row)
    real = jnp.logical_and(lane < faces * PAD_ROWS, lane % PAD_ROWS < elements)
    return jnp.where(real, row, -1)


def contract(left, right):
    return lax.dot_general(left, right, (((1,), (1,)), ((), ())), preferred_element_type=F32)


def store_sent(target_row, faces_ref, tails_ref, section, out_ref):
    count = faces_ref.shape[0]
    rows = out_ref.shape[0] - PAD_ROWS
    table = (iota((rows, count), 0) + section * rows == target_row[:, 0:count]).astype(BF16)
    out_ref[0:rows] = select_rows(table, faces_ref[:, 0:LANES])
    high, low = split(tails_ref[...])
    tails = contract(high[:, 0:count], table) + contract(low[:, 0:count], table)
    out_ref[rows : rows + TAIL_STEP] = tails[:, 0:LANES]
    out_ref[rows + TAIL_STEP :] = jnp.pad(tails[:, LANES:], ((0, 0), (0, WIDE - rows)))


def store_tails(faces_ref, tails_ref):
    tail = jnp.pad(faces_ref[:, LANES:WIDE], ((0, LANES - faces_ref.shape[0]), (0, 0)))
    tails_ref[...] = jnp.transpose(tail)[0:TAIL_STEP]


def first_kernel(
    ahead, my_part_ref, forcing_hbm, precond_hbm, off_hbm, part_hbm, slot_hbm,
    adjoint_ref, faces_ref, tails_ref, target_ref, next_ref,
    forcing_ref, precond_ref, kept_ref, part_ref, slot_ref, sems, off_sems,
):
    rows = next_ref.shape[0] - PAD_ROWS
    whole = [
        pltpu.make_async_copy(source, target, sems.at[i])
        for i, (source, target) in enumerate(
            (
                (forcing_hbm, forcing_ref),
                (precond_hbm, precond_ref),
                (part_hbm, part_ref),
                (slot_hbm, slot_ref),
            )
        )
    ]
    by_element = [
        pltpu.make_async_copy(off_hbm.at[e], kept_ref.at[e], off_sems.at[e])
        for e in range(off_hbm.shape[0])
    ]
    for copy in whole + by_element[:ahead]:
        copy.start()
    adjoint_ref[...] = jnp.zeros(adjoint_ref.shape, F32)
    for copy in whole:
        copy.wait()
    target = face_targets(part_ref, slot_ref, my_part_ref[0], rows)
    target_ref[...] = target
    block_products(forcing_ref, precond_ref, adjoint_ref)

    def arrived(e):
        if e + ahead < len(by_element):
            by_element[e + ahead].start()
        by_element[e].wait()

    face_products(adjoint_ref, kept_ref, faces_ref, arrived)
    store_tails(faces_ref, tails_ref)
    store_sent(target, faces_ref, tails_ref, 2, next_ref)


def chip_kernel(faces_ref, tails_ref, target_ref, chip_ref):
    store_sent(target_ref[...], faces_ref, tails_ref, 1, chip_ref)


def own_part(
    forcing_ref, adjoint_ref, diag_ref, faces_ref, tails_ref, target_ref, own_ref, rest_ref, arrived
):
    elements, width = forcing_ref.shape
    store_sent(target_ref[...], faces_ref, tails_ref, 0, own_ref)
    rest_ref[...] = jnp.zeros(rest_ref.shape, F32)
    arrived()
    block_products(adjoint_ref, diag_ref, rest_ref)
    rest_ref[0:elements, 0:width] = forcing_ref[...] - rest_ref[0:elements, 0:width]


def own_kernel_first(
    forcing_ref, adjoint_ref, diag_hbm, faces_ref, tails_ref, target_ref, perm_hbm,
    own_ref, rest_ref, place_ref, diag_ref, perm_ref, sems,
):
    copies = [
        pltpu.make_async_copy(perm_hbm, perm_ref, sems.at[0]),
        pltpu.make_async_copy(diag_hbm, diag_ref, sems.at[1]),
    ]
    for copy in copies:
        copy.start()
    own_part(
        forcing_ref, adjoint_ref, diag_ref, faces_ref, tails_ref, target_ref, own_ref, rest_ref,
        lambda: [copy.wait() for copy in copies],
    )
    elements = forcing_ref.shape[0]
    perm = perm_ref[...]
    rank = (perm * (65536 // elements + 1)) >> 16
    place = rank * PAD_ROWS + perm - rank * elements
    place_ref[...] = (iota(place_ref.shape, 0) == place).astype(F32).astype(BF16)


def own_kernel_next(
    forcing_ref, adjoint_ref, diag_ref, faces_ref, tails_ref, target_ref, own_ref, rest_ref
):
    own_part(
        forcing_ref, adjoint_ref, diag_ref, faces_ref, tails_ref, target_ref, own_ref, rest_ref,
        lambda: None,
    )


def pack_kernel(own_ref, chip_ref, next_ref, place_ref, out_ref):
    ranks = out_ref.shape[0]
    rows = own_ref.shape[0] - PAD_ROWS
    total = own_ref[...] + chip_ref[...] + next_ref[...]
    place = place_ref[...]
    main = select_rows(place, total[0:rows])
    tails = jnp.concatenate([total[rows : rows + TAIL_STEP], total[rows + TAIL_STEP :]], axis=1)
    high, low = split(jnp.pad(tails[:, 0:rows], ((0, LANES - TAIL_STEP), (0, 0))))
    tail = contract(place, high) + contract(place, low)
    moved = pltpu.roll(tail, 0, 1, stride=TAIL_STEP, stride_axis=0)
    row = iota((PAD_ROWS, LANES), 0)
    for r in range(ranks):
        at = slice(r * PAD_ROWS, (r + 1) * PAD_ROWS)
        packed = jnp.sum(moved[at], axis=0, keepdims=True)
        out_ref[r] = jnp.where(row == PAD_ROWS - 4, packed, main[at])


def gathered_rows(arrived_ref, width):
    total = arrived_ref[0]
    for r in range(1, arrived_ref.shape[0]):
        total = total + arrived_ref[r]
    packed = total[PAD_ROWS - 4 : PAD_ROWS - 3]
    tail = jnp.broadcast_to(packed, (PAD_ROWS, LANES))
    row = iota((PAD_ROWS, LANES), 0)
    for r in range(1, PAD_ROWS - 4):
        tail = jnp.where(row == r, pltpu.roll(packed, LANES - TAIL_STEP * r, 1), tail)
    tail = jnp.where(iota((PAD_ROWS, LANES), 1) < width - LANES, tail, 0.0)
    return jnp.concatenate([total, tail], axis=1)


def next_kernel(
    arrived_ref, rest_ref, before_ref, precond_ref, blocks_ref, target_ref,
    adjoint_ref, faces_ref, tails_ref, next_ref, residual_ref,
):
    width = precond_ref.shape[-1]
    residual_ref[...] = rest_ref[...] - gathered_rows(arrived_ref, width)
    adjoint_ref[...] = jnp.zeros(adjoint_ref.shape, F32)
    block_products(residual_ref, precond_ref, adjoint_ref)
    adjoint_ref[...] = before_ref[...] + adjoint_ref[...]
    face_products(adjoint_ref, blocks_ref, faces_ref, lambda e: None)
    store_tails(faces_ref, tails_ref)
    store_sent(target_ref[...], faces_ref, tails_ref, 2, next_ref)


def last_kernel(
    arrived_ref, rest_ref, before_ref, precond_ref, adjoint_ref, residual_ref, held_ref, sum_ref
):
    elements, width = residual_ref.shape
    held_ref[...] = rest_ref[...] - gathered_rows(arrived_ref, width)
    residual_ref[...] = held_ref[0:elements, 0:width]
    block_products(held_ref, precond_ref, sum_ref)
    adjoint_ref[...] = before_ref[0:elements, 0:width] + sum_ref[0:elements, 0:width]


def in_hbm(*arrays):
    return [pltpu.with_memory_space_constraint(a, pltpu.HBM) for a in arrays]


def cost(flops):
    return pl.CostEstimate(flops=flops, bytes_accessed=1 << 20, transcendentals=0)


def make_calls(elements, faces, width, ranks, ahead=6):
    part_rows = elements * ranks
    vector = pltpu.VMEM((PAD_ROWS, WIDE), F32)
    sent = pltpu.VMEM((part_rows + PAD_ROWS, LANES), F32)
    face_rows = pltpu.VMEM((faces * PAD_ROWS, WIDE), F32)
    tails = pltpu.VMEM((TAIL_STEP, LANES), F32)
    target = pltpu.VMEM((1, LANES), jnp.int32)
    hbm = pl.BlockSpec(memory_space=pltpu.HBM)
    smem = pl.BlockSpec(memory_space=pltpu.SMEM)
    vmem = pl.BlockSpec(memory_space=pltpu.VMEM)
    out = jax.ShapeDtypeStruct((elements, width), F32)
    blocks = pltpu.VMEM((elements, width, width), BF16)
    kept = (
        pltpu.VMEM((elements, width), F32),
        blocks,
        pltpu.VMEM((elements, faces, width, width), BF16),
    )
    indices = pltpu.VMEM((faces, elements), jnp.int32)
    first = pl.pallas_call(
        functools.partial(first_kernel, ahead),
        out_shape=(vector, face_rows, tails, target, sent, *kept),
        in_specs=[smem] + [hbm] * 5,
        scratch_shapes=[
            indices,
            indices,
            pltpu.SemaphoreType.DMA((4,)),
            pltpu.SemaphoreType.DMA((elements,)),
        ],
        compiler_params=PARAMS,
        name="first",
    )
    chip = pl.pallas_call(
        chip_kernel,
        out_shape=sent,
        compiler_params=PARAMS,
        name="chip",
    )
    own_first = pl.pallas_call(
        own_kernel_first,
        out_shape=(sent, vector, pltpu.VMEM((ranks * PAD_ROWS, part_rows), BF16), blocks),
        in_specs=[vmem, vmem, hbm, vmem, vmem, vmem, hbm],
        scratch_shapes=[pltpu.VMEM((1, part_rows), jnp.int32), pltpu.SemaphoreType.DMA((2,))],
        compiler_params=PARAMS,
        cost_estimate=cost(10**9),
        name="own_first",
    )
    own_next = pl.pallas_call(
        own_kernel_next,
        out_shape=(sent, vector),
        compiler_params=PARAMS,
        cost_estimate=cost(10**9),
        name="own_next",
    )
    pack = pl.pallas_call(
        pack_kernel,
        out_shape=pltpu.VMEM((ranks, PAD_ROWS, LANES), F32),
        compiler_params=PARAMS,
        name="pack",
    )
    following = pl.pallas_call(
        next_kernel,
        out_shape=(vector, face_rows, tails, sent),
        scratch_shapes=[vector],
        compiler_params=PARAMS,
        name="following",
    )
    last = pl.pallas_call(
        last_kernel,
        out_shape=(out, out),
        scratch_shapes=[vector] * 2,
        compiler_params=PARAMS,
        name="last",
    )
    return first, chip, own_first, own_next, pack, following, last


def shards(forcing, diag_blocks, off_blocks, precond, face_part, face_slot, row_perm):
    elements, width = forcing.shape
    faces = face_part.shape[0]
    ranks = lax.axis_size("grp")
    parts = lax.axis_size("dom")
    first, chip, own_first, own_next, pack, following, last = make_calls(
        elements, faces, width, ranks
    )
    my_part = lax.axis_index("dom").astype(jnp.int32).reshape(1)
    on_chip = [(p, p ^ 1) for p in range(parts)]
    across = [(p, ((p + 1) ^ 1) - 1) for p in range(1, parts - 1)]
    forcing, precond, off_blocks, diag_blocks, face_part, face_slot, row_perm = in_hbm(
        forcing, precond, off_blocks, diag_blocks, face_part, face_slot, row_perm
    )

    def exchange(beyond, face_terms):
        from_beyond = lax.ppermute(beyond, "dom", across)
        sent = chip(*face_terms, target)
        return from_beyond, lax.ppermute(sent, "dom", on_chip)

    adjoint, *face_terms, target, beyond, forcing, precond, kept = first(
        my_part, forcing, precond, off_blocks, face_part, face_slot
    )
    from_beyond, from_chip = exchange(beyond, face_terms)
    own, rest, place, diag_blocks = own_first(
        forcing, adjoint, diag_blocks, *face_terms, target, row_perm
    )
    arrived = lax.all_to_all(pack(own, from_chip, from_beyond, place), "grp", 0, 0)

    adjoint, *face_terms, beyond = following(arrived, rest, adjoint, precond, kept, target)
    from_beyond, from_chip = exchange(beyond, face_terms)
    own, rest = own_next(forcing, adjoint, diag_blocks, *face_terms, target)
    arrived = lax.all_to_all(pack(own, from_chip, from_beyond, place), "grp", 0, 0)
    return last(arrived, rest, adjoint, precond)


def solution(mesh):
    return jax.shard_map(
        shards,
        mesh=mesh,
        in_specs=(
            P(("dom", "grp"), None),
            P(("dom", "grp"), None, None),
            P(("dom", "grp"), None, None, None),
            P(("dom", "grp"), None, None),
            P(None, ("dom", "grp")),
            P(None, ("dom", "grp")),
            P("dom", None),
        ),
        out_specs=(P(("dom", "grp"), None), P(("dom", "grp"), None)),
        check_vma=False,
    )
```

```python
import functools

import jax
import jax.numpy as jnp
from jax import lax
from jax.experimental import pallas as pl
from jax.experimental.pallas import tpu as pltpu
from jax.sharding import PartitionSpec as P

LANES = 128
WIDE = 256
PAD_ROWS = 16
TAIL_STEP = 8
F32 = jnp.float32
BF16 = jnp.bfloat16
PARAMS = pltpu.CompilerParams(vmem_limit_bytes=16 * 1024 * 1024)


def iota(shape, axis):
    return lax.broadcasted_iota(jnp.int32, shape, axis)


def split(values):
    high = values.astype(BF16)
    return high, (values - high.astype(F32)).astype(BF16)


def contract(left, right):
    return lax.dot_general(left, right, (((1,), (1,)), ((), ())), preferred_element_type=F32)


def block_products(vector_ref, blocks_ref, out_ref):
    elements, width = blocks_ref.shape[0], blocks_ref.shape[-1]
    for e in range(elements):
        row = vector_ref[e : e + 1, 0:width].astype(BF16)
        out_ref[e : e + 1, 0:width] = jnp.dot(row, blocks_ref[e], preferred_element_type=F32)


def face_products(adjoint_ref, blocks_ref, sent_ref, tails_ref, arrived):
    elements, faces, width = blocks_ref.shape[0], blocks_ref.shape[1], blocks_ref.shape[-1]
    tails_ref[...] = jnp.zeros(tails_ref.shape, F32)
    for e in range(elements):
        row = adjoint_ref[e : e + 1, 0:width].astype(BF16)
        arrived(e)
        for k in range(faces):
            at = k * elements + e
            product = jnp.dot(row, blocks_ref[e, k], preferred_element_type=F32)
            sent_ref[at : at + 1, :] = product[:, 0:LANES]
            tails_ref[at : at + 1, 0 : width - LANES] = product[:, LANES:width]
    count = faces * elements
    sent_ref[count : count + TAIL_STEP, :] = jnp.transpose(tails_ref[...])[0:TAIL_STEP]


def face_targets(part_ref, slot_ref, my_part, part_rows):
    faces, elements = part_ref.shape
    part, slot = part_ref[...], slot_ref[...]
    offset = part - my_part
    towards_chip = 1 - 2 * (my_part & 1)
    section = jnp.where(offset == 0, 0, jnp.where(offset == towards_chip, 1, 2))
    target = jnp.where(part < 0, -1, section * part_rows + slot)
    target = jnp.pad(target, ((0, 0), (0, LANES - elements)))
    row = jnp.full((1, LANES), -1, jnp.int32)
    lane = iota((1, LANES), 1)
    for k in range(faces):
        moved = pltpu.roll(target[k : k + 1], k * elements, 1)
        inside = jnp.logical_and(lane >= k * elements, lane < (k + 1) * elements)
        row = jnp.where(inside, moved, row)
    return row


def store_target(target_row, sent_ref, count):
    row = jnp.broadcast_to(target_row.astype(F32), (TAIL_STEP, LANES))
    sent_ref[count + TAIL_STEP :, :] = row


def first_kernel(
    ahead, my_part_ref, forcing_hbm, precond_hbm, off_hbm, diag_hbm, part_hbm, slot_hbm, perm_hbm,
    adjoint_ref, sent_ref, target_ref, place_ref,
    forcing_ref, precond_ref, kept_ref, diag_ref,
    part_ref, slot_ref, perm_ref, tails_ref, sems, off_sems,
):
    part_rows = perm_ref.shape[1]
    faces, elements = part_ref.shape
    whole = [
        pltpu.make_async_copy(source, target, sems.at[i])
        for i, (source, target) in enumerate(
            (
                (forcing_hbm, forcing_ref),
                (precond_hbm, precond_ref),
                (part_hbm, part_ref),
                (slot_hbm, slot_ref),
                (perm_hbm, perm_ref),
            )
        )
    ]
    diag_copy = pltpu.make_async_copy(diag_hbm, diag_ref, sems.at[5])
    queue = [
        pltpu.make_async_copy(off_hbm.at[e], kept_ref.at[e], off_sems.at[e])
        for e in range(elements)
    ] + [diag_copy]
    for copy in whole + queue[:ahead]:
        copy.start()
    adjoint_ref[...] = jnp.zeros(adjoint_ref.shape, F32)
    for copy in whole:
        copy.wait()
    block_products(forcing_ref, precond_ref, adjoint_ref)
    perm = perm_ref[...]
    rank = (perm * (65536 // elements + 1)) >> 16
    place_ref[...] = rank * PAD_ROWS + perm - rank * elements + 1
    target = face_targets(part_ref, slot_ref, my_part_ref[0], part_rows)
    target_ref[...] = target
    store_target(target, sent_ref, faces * elements)

    def arrived(e):
        if e + ahead < len(queue):
            queue[e + ahead].start()
        queue[e].wait()

    face_products(adjoint_ref, kept_ref, sent_ref, tails_ref, arrived)
    diag_copy.wait()


def rest_kernel(forcing_ref, adjoint_ref, diag_ref, rest_ref):
    elements, width = forcing_ref.shape
    rest_ref[...] = jnp.zeros(rest_ref.shape, F32)
    block_products(adjoint_ref, diag_ref, rest_ref)
    rest_ref[0:elements, 0:width] = forcing_ref[...] - rest_ref[0:elements, 0:width]


def pack_rows(buffers, table, rows_ref, out_ref):
    count = buffers[0].shape[0] - 2 * TAIL_STEP
    ranks = out_ref.shape[0]
    rows_ref[...] = jnp.zeros(rows_ref.shape, F32)
    tails = jnp.zeros((TAIL_STEP, WIDE), F32)
    for i, buffer in enumerate(buffers):
        rows_ref[i * count : (i + 1) * count, :] = buffer[0:count, :]
        tail = jnp.pad(buffer[count : count + TAIL_STEP, :], ((0, 0), (0, WIDE - LANES)))
        tails = tails + (pltpu.roll(tail, i * count, 1) if i else tail)
    high, low = split(rows_ref[...])
    main = jnp.dot(table, high, preferred_element_type=F32) + jnp.dot(
        table, low, preferred_element_type=F32
    )
    high, low = split(jnp.pad(tails, ((0, LANES - TAIL_STEP), (0, 0))))
    tail = contract(table, high) + contract(table, low)
    moved = pltpu.roll(tail, 0, 1, stride=TAIL_STEP, stride_axis=0)
    row = iota((PAD_ROWS, LANES), 0)
    for r in range(ranks):
        at = slice(r * PAD_ROWS, (r + 1) * PAD_ROWS)
        packed = jnp.sum(moved[at], axis=0, keepdims=True)
        out_ref[r] = jnp.where(row == PAD_ROWS - 4, packed, main[at])


def pack_kernel_first(
    own_ref, chip_ref, next_ref, target_ref, place_ref, out_ref, table_ref, rows_ref
):
    count = own_ref.shape[0] - 2 * TAIL_STEP
    part_rows = place_ref.shape[1]
    lane = iota((1, WIDE), 1)
    wanted = jnp.full((1, WIDE), -1, jnp.int32)
    for i, target in enumerate(
        (
            target_ref[...],
            chip_ref[count + TAIL_STEP : count + TAIL_STEP + 1, :].astype(jnp.int32),
            next_ref[count + TAIL_STEP : count + TAIL_STEP + 1, :].astype(jnp.int32),
        )
    ):
        slot = jnp.pad(target - i * part_rows, ((0, 0), (0, WIDE - LANES)))
        slot = pltpu.roll(slot, i * count, 1) if i else slot
        inside = jnp.logical_and(lane >= i * count, lane < (i + 1) * count)
        wanted = jnp.where(inside, slot, wanted)
    slots = (iota((part_rows, WIDE), 0) == wanted).astype(F32).astype(BF16)
    place = jnp.broadcast_to(place_ref[...].astype(F32), (TAIL_STEP, part_rows)).astype(BF16)
    position = jnp.dot(place, slots, preferred_element_type=F32)[0:1].astype(jnp.int32)
    table = (iota(table_ref.shape, 0) + 1 == position).astype(F32).astype(BF16)
    table_ref[...] = table
    pack_rows((own_ref, chip_ref, next_ref), table, rows_ref, out_ref)


def pack_kernel_next(own_ref, chip_ref, next_ref, table_ref, out_ref, rows_ref):
    pack_rows((own_ref, chip_ref, next_ref), table_ref[...], rows_ref, out_ref)


def gathered_rows(arrived_ref, width):
    total = arrived_ref[0]
    for r in range(1, arrived_ref.shape[0]):
        total = total + arrived_ref[r]
    packed = total[PAD_ROWS - 4 : PAD_ROWS - 3]
    tail = jnp.broadcast_to(packed, (PAD_ROWS, LANES))
    row = iota((PAD_ROWS, LANES), 0)
    for r in range(1, PAD_ROWS - 4):
        tail = jnp.where(row == r, pltpu.roll(packed, LANES - TAIL_STEP * r, 1), tail)
    tail = jnp.where(iota((PAD_ROWS, LANES), 1) < width - LANES, tail, 0.0)
    return jnp.concatenate([total, tail], axis=1)


def next_kernel(
    arrived_ref, rest_ref, before_ref, precond_ref, blocks_ref, target_ref,
    adjoint_ref, sent_ref, residual_ref, tails_ref,
):
    elements, faces, width = blocks_ref.shape[:3]
    residual_ref[...] = rest_ref[...] - gathered_rows(arrived_ref, width)
    adjoint_ref[...] = jnp.zeros(adjoint_ref.shape, F32)
    block_products(residual_ref, precond_ref, adjoint_ref)
    adjoint_ref[...] = before_ref[...] + adjoint_ref[...]
    store_target(target_ref[...], sent_ref, faces * elements)
    face_products(adjoint_ref, blocks_ref, sent_ref, tails_ref, lambda e: None)


def last_kernel(
    arrived_ref, rest_ref, before_ref, precond_ref, adjoint_ref, residual_ref, held_ref, sum_ref
):
    elements, width = residual_ref.shape
    held_ref[...] = rest_ref[...] - gathered_rows(arrived_ref, width)
    residual_ref[...] = held_ref[0:elements, 0:width]
    block_products(held_ref, precond_ref, sum_ref)
    adjoint_ref[...] = before_ref[0:elements, 0:width] + sum_ref[0:elements, 0:width]


def in_hbm(*arrays):
    return [pltpu.with_memory_space_constraint(a, pltpu.HBM) for a in arrays]


def cost(flops):
    return pl.CostEstimate(flops=flops, bytes_accessed=1 << 20, transcendentals=0)


def make_calls(elements, faces, width, ranks, ahead=6):
    part_rows = elements * ranks
    vector = pltpu.VMEM((PAD_ROWS, WIDE), F32)
    sent = pltpu.VMEM((faces * elements + 2 * TAIL_STEP, LANES), F32)
    tails = pltpu.VMEM((LANES, LANES), F32)
    hbm = pl.BlockSpec(memory_space=pltpu.HBM)
    smem = pl.BlockSpec(memory_space=pltpu.SMEM)
    out = jax.ShapeDtypeStruct((elements, width), F32)
    blocks = pltpu.VMEM((elements, width, width), BF16)
    perm = pltpu.VMEM((1, part_rows), jnp.int32)
    kept = (
        pltpu.VMEM((elements, width), F32),
        blocks,
        pltpu.VMEM((elements, faces, width, width), BF16),
        blocks,
    )
    indices = pltpu.VMEM((faces, elements), jnp.int32)
    packed = pltpu.VMEM((ranks, PAD_ROWS, LANES), F32)
    rows = pltpu.VMEM((WIDE, LANES), F32)
    table = pltpu.VMEM((ranks * PAD_ROWS, WIDE), BF16)
    first = pl.pallas_call(
        functools.partial(first_kernel, ahead),
        out_shape=(vector, sent, pltpu.VMEM((1, LANES), jnp.int32), perm, *kept),
        in_specs=[smem] + [hbm] * 7,
        scratch_shapes=[
            indices,
            indices,
            perm,
            tails,
            pltpu.SemaphoreType.DMA((6,)),
            pltpu.SemaphoreType.DMA((elements,)),
        ],
        compiler_params=PARAMS,
        name="first",
    )
    rest = pl.pallas_call(
        rest_kernel,
        out_shape=vector,
        compiler_params=PARAMS,
        cost_estimate=cost(10**9),
        name="rest",
    )
    pack_first = pl.pallas_call(
        pack_kernel_first,
        out_shape=(packed, table),
        scratch_shapes=[rows],
        compiler_params=PARAMS,
        name="pack_first",
    )
    pack_next = pl.pallas_call(
        pack_kernel_next,
        out_shape=packed,
        scratch_shapes=[rows],
        compiler_params=PARAMS,
        name="pack_next",
    )
    following = pl.pallas_call(
        next_kernel,
        out_shape=(vector, sent),
        scratch_shapes=[vector, tails],
        compiler_params=PARAMS,
        name="following",
    )
    last = pl.pallas_call(
        last_kernel,
        out_shape=(out, out),
        scratch_shapes=[vector] * 2,
        compiler_params=PARAMS,
        name="last",
    )
    return first, rest, pack_first, pack_next, following, last


def shards(forcing, diag_blocks, off_blocks, precond, face_part, face_slot, row_perm):
    elements, width = forcing.shape
    faces = face_part.shape[0]
    ranks = lax.axis_size("grp")
    parts = lax.axis_size("dom")
    first, rest_of, pack_first, pack_next, following, last = make_calls(
        elements, faces, width, ranks
    )
    my_part = lax.axis_index("dom").astype(jnp.int32).reshape(1)
    on_chip = [(p, p ^ 1) for p in range(parts)]
    across = [(p, ((p + 1) ^ 1) - 1) for p in range(1, parts - 1)]

    def exchange(sent, *rest_operands):
        from_beyond = lax.ppermute(sent, "dom", across)
        from_chip = lax.ppermute(sent, "dom", on_chip)
        return from_chip, from_beyond, rest_of(*rest_operands)

    adjoint, sent, target, place, forcing, precond, kept, diag_blocks = first(
        my_part,
        *in_hbm(forcing, precond, off_blocks, diag_blocks, face_part, face_slot, row_perm),
    )
    *received, rest = exchange(sent, forcing, adjoint, diag_blocks)
    outgoing, table = pack_first(sent, *received, target, place)
    arrived = lax.all_to_all(outgoing, "grp", 0, 0)

    adjoint, sent = following(arrived, rest, adjoint, precond, kept, target)
    *received, rest = exchange(sent, forcing, adjoint, diag_blocks)
    arrived = lax.all_to_all(pack_next(sent, *received, table), "grp", 0, 0)
    return last(arrived, rest, adjoint, precond)


def solution(mesh):
    return jax.shard_map(
        shards,
        mesh=mesh,
        in_specs=(
            P(("dom", "grp"), None),
            P(("dom", "grp"), None, None),
            P(("dom", "grp"), None, None, None),
            P(("dom", "grp"), None, None),
            P(None, ("dom", "grp")),
            P(None, ("dom", "grp")),
            P("dom", None),
        ),
        out_specs=(P(("dom", "grp"), None), P(("dom", "grp"), None)),
        check_vma=False,
    )
```

```python
import functools

import jax
import jax.numpy as jnp
from jax import lax
from jax.experimental import pallas as pl
from jax.experimental.pallas import tpu as pltpu
from jax.sharding import PartitionSpec as P

LANES = 128
WIDE = 256
PAD_ROWS = 16
TAIL_STEP = 8
F32 = jnp.float32
BF16 = jnp.bfloat16
PARAMS = pltpu.CompilerParams(vmem_limit_bytes=16 * 1024 * 1024)


def iota(shape, axis):
    return lax.broadcasted_iota(jnp.int32, shape, axis)


def split(values):
    high = values.astype(BF16)
    return high, (values - high.astype(F32)).astype(BF16)


def contract(left, right):
    return lax.dot_general(left, right, (((1,), (1,)), ((), ())), preferred_element_type=F32)


def block_products(vector_ref, blocks_ref, out_ref):
    elements, width = blocks_ref.shape[0], blocks_ref.shape[-1]
    for e in range(elements):
        row = vector_ref[e : e + 1, 0:width].astype(BF16)
        out_ref[e : e + 1, 0:width] = jnp.dot(row, blocks_ref[e], preferred_element_type=F32)


def face_products(adjoint_ref, blocks_ref, sent_ref, tails_ref, arrived):
    elements, faces, width = blocks_ref.shape[0], blocks_ref.shape[1], blocks_ref.shape[-1]
    tails_ref[...] = jnp.zeros(tails_ref.shape, F32)
    for e in range(elements):
        row = adjoint_ref[e : e + 1, 0:width].astype(BF16)
        arrived(e)
        for k in range(faces):
            at = k * elements + e
            product = jnp.dot(row, blocks_ref[e, k], preferred_element_type=F32)
            sent_ref[at : at + 1, :] = product[:, 0:LANES]
            tails_ref[at : at + 1, 0 : width - LANES] = product[:, LANES:width]
    count = faces * elements
    sent_ref[count : count + TAIL_STEP, :] = jnp.transpose(tails_ref[...])[0:TAIL_STEP]


def face_targets(part_ref, slot_ref, my_part, part_rows):
    faces, elements = part_ref.shape
    part, slot = part_ref[...], slot_ref[...]
    my_part = my_part[:, 0:elements]
    offset = part - my_part
    towards_chip = 1 - 2 * (my_part & 1)
    section = jnp.where(offset == 0, 0, jnp.where(offset == towards_chip, 1, 2))
    target = jnp.where(part < 0, -1, section * part_rows + slot)
    target = jnp.pad(target, ((0, 0), (0, LANES - elements)))
    row = jnp.full((1, LANES), -1, jnp.int32)
    lane = iota((1, LANES), 1)
    for k in range(faces):
        moved = pltpu.roll(target[k : k + 1], k * elements, 1)
        inside = jnp.logical_and(lane >= k * elements, lane < (k + 1) * elements)
        row = jnp.where(inside, moved, row)
    return row


def store_target(target_row, sent_ref, count):
    row = jnp.broadcast_to(target_row.astype(F32), (TAIL_STEP, LANES))
    sent_ref[count + TAIL_STEP :, :] = row


def first_kernel(
    ahead, my_part_ref, forcing_hbm, precond_hbm, off_hbm, diag_hbm, part_hbm, slot_hbm, perm_hbm,
    adjoint_ref, sent_ref, target_ref, place_ref,
    forcing_ref, precond_ref, kept_ref, diag_ref,
    part_ref, slot_ref, perm_ref, tails_ref, sems, off_sems,
):
    part_rows = perm_ref.shape[1]
    faces, elements = part_ref.shape
    whole = [
        pltpu.make_async_copy(source, target, sems.at[i])
        for i, (source, target) in enumerate(
            (
                (forcing_hbm, forcing_ref),
                (precond_hbm, precond_ref),
                (part_hbm, part_ref),
                (slot_hbm, slot_ref),
                (perm_hbm, perm_ref),
            )
        )
    ]
    diag_copy = pltpu.make_async_copy(diag_hbm, diag_ref, sems.at[5])
    chunk = elements // off_sems.shape[0]
    queue = [
        pltpu.make_async_copy(
            off_hbm.at[pl.ds(e, chunk)], kept_ref.at[pl.ds(e, chunk)], off_sems.at[e // chunk]
        )
        for e in range(0, elements, chunk)
    ] + [diag_copy]
    early, ahead, _ = ahead
    for copy in whole + queue[:early]:
        copy.start()
    adjoint_ref[...] = jnp.zeros(adjoint_ref.shape, F32)
    for copy in whole:
        copy.wait()
    for copy in queue[early:ahead]:
        copy.start()
    block_products(forcing_ref, precond_ref, adjoint_ref)
    perm = perm_ref[...]
    rank = (perm * (65536 // elements + 1)) >> 16
    place_ref[...] = rank * PAD_ROWS + perm - rank * elements + 1
    target = face_targets(part_ref, slot_ref, my_part_ref[...], part_rows)
    target_ref[...] = target
    store_target(target, sent_ref, faces * elements)

    def arrived(e):
        if e % chunk == 0:
            if e // chunk + ahead < len(queue):
                queue[e // chunk + ahead].start()
            queue[e // chunk].wait()

    face_products(adjoint_ref, kept_ref, sent_ref, tails_ref, arrived)
    diag_copy.wait()


def rest_kernel(forcing_ref, adjoint_ref, diag_ref, rest_ref):
    elements, width = forcing_ref.shape
    rest_ref[...] = jnp.zeros(rest_ref.shape, F32)
    block_products(adjoint_ref, diag_ref, rest_ref)
    rest_ref[0:elements, 0:width] = forcing_ref[...] - rest_ref[0:elements, 0:width]


def pack_rows(buffers, table, rows_ref, out_ref):
    count = buffers[0].shape[0] - 2 * TAIL_STEP
    ranks = out_ref.shape[0]
    used = len(buffers) * count
    rows_ref[used:, :] = jnp.zeros((WIDE - used, LANES), F32)
    tails = jnp.zeros((TAIL_STEP, WIDE), F32)
    for i, buffer in enumerate(buffers):
        rows_ref[i * count : (i + 1) * count, :] = buffer[0:count, :]
        tail = jnp.pad(buffer[count : count + TAIL_STEP, :], ((0, 0), (0, WIDE - LANES)))
        tails = tails + (pltpu.roll(tail, i * count, 1) if i else tail)
    both = jnp.dot(
        table, jnp.concatenate(split(rows_ref[...]), axis=1), preferred_element_type=F32
    )
    main = both[:, 0:LANES] + both[:, LANES:WIDE]
    high, low = split(jnp.pad(tails, ((0, LANES - TAIL_STEP), (0, 0))))
    both = contract(table, jnp.concatenate([high, low], axis=0))
    tail = both[:, 0:LANES] + both[:, LANES:WIDE]
    moved = pltpu.roll(tail, 0, 1, stride=TAIL_STEP, stride_axis=0)
    row = iota((PAD_ROWS, LANES), 0)
    for r in range(ranks):
        at = slice(r * PAD_ROWS, (r + 1) * PAD_ROWS)
        packed = jnp.sum(moved[at], axis=0, keepdims=True)
        out_ref[r] = jnp.where(row == PAD_ROWS - 4, packed, main[at])


def pack_kernel_first(
    own_ref, chip_ref, next_ref, target_ref, place_ref, out_ref, table_ref, rows_ref
):
    count = own_ref.shape[0] - 2 * TAIL_STEP
    part_rows = place_ref.shape[1]
    lane = iota((1, WIDE), 1)
    wanted = jnp.full((1, WIDE), -1, jnp.int32)
    for i, target in enumerate(
        (
            target_ref[...],
            chip_ref[count + TAIL_STEP : count + TAIL_STEP + 1, :].astype(jnp.int32),
            next_ref[count + TAIL_STEP : count + TAIL_STEP + 1, :].astype(jnp.int32),
        )
    ):
        slot = jnp.pad(target - i * part_rows, ((0, 0), (0, WIDE - LANES)))
        slot = pltpu.roll(slot, i * count, 1) if i else slot
        inside = jnp.logical_and(lane >= i * count, lane < (i + 1) * count)
        wanted = jnp.where(inside, slot, wanted)
    slots = (iota((part_rows, WIDE), 0) == wanted).astype(F32).astype(BF16)
    place = jnp.broadcast_to(place_ref[...].astype(F32), (TAIL_STEP, part_rows)).astype(BF16)
    position = jnp.dot(place, slots, preferred_element_type=F32)[0:1].astype(jnp.int32)
    table = (iota(table_ref.shape, 0) + 1 == position).astype(F32).astype(BF16)
    table_ref[...] = table
    pack_rows((own_ref, chip_ref, next_ref), table, rows_ref, out_ref)


def pack_kernel_next(own_ref, chip_ref, next_ref, table_ref, out_ref, rows_ref):
    pack_rows((own_ref, chip_ref, next_ref), table_ref[...], rows_ref, out_ref)


def gathered_rows(arrived_ref, width):
    total = arrived_ref[0]
    for r in range(1, arrived_ref.shape[0]):
        total = total + arrived_ref[r]
    packed = total[PAD_ROWS - 4 : PAD_ROWS - 3]
    tail = jnp.broadcast_to(packed, (PAD_ROWS, LANES))
    row = iota((PAD_ROWS, LANES), 0)
    for r in range(1, PAD_ROWS - 4):
        tail = jnp.where(row == r, pltpu.roll(packed, LANES - TAIL_STEP * r, 1), tail)
    tail = jnp.where(iota((PAD_ROWS, LANES), 1) < width - LANES, tail, 0.0)
    return jnp.concatenate([total, tail], axis=1)


def next_kernel(
    arrived_ref, rest_ref, before_ref, precond_ref, blocks_ref, target_ref,
    adjoint_ref, sent_ref, residual_ref, tails_ref,
):
    elements, faces, width = blocks_ref.shape[:3]
    residual_ref[...] = rest_ref[...] - gathered_rows(arrived_ref, width)
    adjoint_ref[...] = jnp.zeros(adjoint_ref.shape, F32)
    block_products(residual_ref, precond_ref, adjoint_ref)
    adjoint_ref[...] = before_ref[...] + adjoint_ref[...]
    store_target(target_ref[...], sent_ref, faces * elements)
    face_products(adjoint_ref, blocks_ref, sent_ref, tails_ref, lambda e: None)


def last_kernel(
    arrived_ref, rest_ref, before_ref, precond_ref, adjoint_ref, residual_ref, held_ref, sum_ref
):
    elements, width = residual_ref.shape
    held_ref[...] = rest_ref[...] - gathered_rows(arrived_ref, width)
    residual_ref[...] = held_ref[0:elements, 0:width]
    block_products(held_ref, precond_ref, sum_ref)
    adjoint_ref[...] = before_ref[0:elements, 0:width] + sum_ref[0:elements, 0:width]


def in_hbm(*arrays):
    return [pltpu.with_memory_space_constraint(a, pltpu.HBM) for a in arrays]


def cost(flops):
    return pl.CostEstimate(flops=flops, bytes_accessed=1 << 20, transcendentals=0)


def make_calls(elements, faces, width, ranks, ahead=(4, 5, 3)):
    part_rows = elements * ranks
    vector = pltpu.VMEM((PAD_ROWS, WIDE), F32)
    sent = pltpu.VMEM((faces * elements + 2 * TAIL_STEP, LANES), F32)
    tails = pltpu.VMEM((LANES, LANES), F32)
    hbm = pl.BlockSpec(memory_space=pltpu.HBM)
    vmem = pl.BlockSpec(memory_space=pltpu.VMEM)
    out = jax.ShapeDtypeStruct((elements, width), F32)
    blocks = pltpu.VMEM((elements, width, width), BF16)
    perm = pltpu.VMEM((1, part_rows), jnp.int32)
    kept = (
        pltpu.VMEM((elements, width), F32),
        blocks,
        pltpu.VMEM((elements, faces, width, width), BF16),
        blocks,
    )
    indices = pltpu.VMEM((faces, elements), jnp.int32)
    packed = pltpu.VMEM((ranks, PAD_ROWS, LANES), F32)
    rows = pltpu.VMEM((WIDE, LANES), F32)
    table = pltpu.VMEM((ranks * PAD_ROWS, WIDE), BF16)
    first = pl.pallas_call(
        functools.partial(first_kernel, ahead),
        out_shape=(vector, sent, pltpu.VMEM((1, LANES), jnp.int32), perm, *kept),
        in_specs=[vmem] + [hbm] * 7,
        scratch_shapes=[
            indices,
            indices,
            perm,
            tails,
            pltpu.SemaphoreType.DMA((6,)),
            pltpu.SemaphoreType.DMA((elements // ahead[2],)),
        ],
        compiler_params=PARAMS,
        name="first",
    )
    rest = pl.pallas_call(
        rest_kernel,
        out_shape=vector,
        compiler_params=PARAMS,
        cost_estimate=cost(10**9),
        name="rest",
    )
    pack_first = pl.pallas_call(
        pack_kernel_first,
        out_shape=(packed, table),
        scratch_shapes=[rows],
        compiler_params=PARAMS,
        name="pack_first",
    )
    pack_next = pl.pallas_call(
        pack_kernel_next,
        out_shape=packed,
        scratch_shapes=[rows],
        compiler_params=PARAMS,
        name="pack_next",
    )
    following = pl.pallas_call(
        next_kernel,
        out_shape=(vector, sent),
        scratch_shapes=[vector, tails],
        compiler_params=PARAMS,
        name="following",
    )
    last = pl.pallas_call(
        last_kernel,
        out_shape=(out, out),
        scratch_shapes=[vector] * 2,
        compiler_params=PARAMS,
        name="last",
    )
    return first, rest, pack_first, pack_next, following, last


def shards(forcing, diag_blocks, off_blocks, precond, face_part, face_slot, row_perm):
    elements, width = forcing.shape
    faces = face_part.shape[0]
    ranks = lax.axis_size("grp")
    parts = lax.axis_size("dom")
    first, rest_of, pack_first, pack_next, following, last = make_calls(
        elements, faces, width, ranks
    )
    my_part = jnp.full((1, LANES), lax.axis_index("dom"), jnp.int32)
    my_part = pltpu.with_memory_space_constraint(my_part, pltpu.VMEM)
    on_chip = [(p, p ^ 1) for p in range(parts)]
    across = [(p, ((p + 1) ^ 1) - 1) for p in range(1, parts - 1)]

    def exchange(sent, *rest_operands):
        from_beyond = lax.ppermute(sent, "dom", across)
        from_chip = lax.ppermute(sent, "dom", on_chip)
        return from_chip, from_beyond, rest_of(*rest_operands)

    adjoint, sent, target, place, forcing, precond, kept, diag_blocks = first(
        my_part,
        *in_hbm(forcing, precond, off_blocks, diag_blocks, face_part, face_slot, row_perm),
    )
    *received, rest = exchange(sent, forcing, adjoint, diag_blocks)
    outgoing, table = pack_first(sent, *received, target, place)
    arrived = lax.all_to_all(outgoing, "grp", 0, 0)

    adjoint, sent = following(arrived, rest, adjoint, precond, kept, target)
    *received, rest = exchange(sent, forcing, adjoint, diag_blocks)
    arrived = lax.all_to_all(pack_next(sent, *received, table), "grp", 0, 0)
    return last(arrived, rest, adjoint, precond)


def solution(mesh):
    return jax.shard_map(
        shards,
        mesh=mesh,
        in_specs=(
            P(("dom", "grp"), None),
            P(("dom", "grp"), None, None),
            P(("dom", "grp"), None, None, None),
            P(("dom", "grp"), None, None),
            P(None, ("dom", "grp")),
            P(None, ("dom", "grp")),
            P("dom", None),
        ),
        out_specs=(P(("dom", "grp"), None), P(("dom", "grp"), None)),
        check_vma=False,
    )
```
